32 devices in a mesh: groups: 2 (over y), blk: 8 (over z, x), mp: 2 (over core).
Axes of the slice: x: 2, y: 2, z: 4, core: 2. Of those that a mesh axis runs over, the one named last changes fastest.
Arguments:
- probe_vectors: bfloat16 [12, 8, 32, 3584], P('groups', 'blk', None, 'mp'), parts along dimension 0, may hold values from -12 to 12
- unsettled_lookups: bfloat16 [12, 8, 32, 512], P('groups', 'blk', None, 'mp'), parts along dimension 0, may hold values from -6 to 6
- unsettled_payloads: bfloat16 [12, 8, 32, 512], P('groups', 'blk', None, 'mp'), parts along dimension 0, may hold values from -6 to 6
- uncover_ordering: int32 [12, 8, 32], P('groups', 'blk'), parts along dimension 0, may hold values from 0 to 31, each once within a row
- rounds_finished: int32 [12, 8], P('groups', 'blk'), parts along dimension 0, may hold values from 0 to 7
- random_entry_choice: int32 [12, 8, 32], P('groups', 'blk'), parts along dimension 0, may hold values from 0 to 63
- noise_token_keys: bfloat16 [64, 512], P(None, 'mp'), may hold values from -6 to 6
- noise_token_values: bfloat16 [64, 512], P(None, 'mp'), may hold values from -6 to 6
- prefix_key_cache: bfloat16 [2, 8, 32, 512], P('groups', 'blk', None, 'mp'), parts along dimension 0, may hold values from -6 to 6
- prefix_value_cache: bfloat16 [2, 8, 32, 512], P('groups', 'blk', None, 'mp'), parts along dimension 0, may hold values from -6 to 6
- completed_keys: bfloat16 [16, 32, 512], P(('groups', 'blk'), None, 'mp'), parts along dimension 0, may hold values from -6 to 6
- completed_values: bfloat16 [16, 32, 512], P(('groups', 'blk'), None, 'mp'), parts along dimension 0, may hold values from -6 to 6
- committing_index: int32 [2], P('groups'), parts along dimension 0, may hold values from 0 to 7, as said below
Outputs:
- attended: bfloat16 [12, 8, 32, 3584], P('groups', 'blk', None, 'mp'), parts along dimension 0
The draws below stay inside these ranges and needn't reach their ends.
There are 2 independent parts, one for each index of `groups`. The reference program is written for one: setup_inputs(seed, part) draws one part's arguments, and reference() takes and returns one part's arrays. A program takes and returns all parts, laid end to end along the dimension named above; an argument that names none is the same for every part. Nothing has to cross between parts.
Inputs may be any that keep to these rules, and one draw needn't show every extreme that they name: `committing_index`: an index of blk; in every odd part it is the last index, 7.
All inputs are finite; a program needn't handle non-finite values.
Results may differ from the reference program's by a relative error of at most 0.005.
Values may be sent and summed in bfloat16 or wider, within the bound.
No kernel may reach another device: no remote copies, remote signals or barrier semaphores. Data moves between devices by JAX's collectives and lax.ppermute only.
A program may use at most 128 MiB of HBM per device.

```python
import jax
import jax.numpy as jnp
from jax import lax

QUERY_GROUPS = 28
MEMORY_GROUPS = 4
FEATURE_DIM = 128
SPAN_LENGTH = 32
DENOISE_ROUNDS = 8
RANDOM_ROWS = 64
OPEN_ON_LANE = 6
CB = 1
UNMASK = 4
OPEN_COUNT = 48
PREFIX = 256
N_BLK = 8


def draw_committing_index(key, part):
    halfway = jax.random.randint(jax.random.fold_in(key, 11), (1,), 0, N_BLK // 2)
    parity = jnp.asarray(part, jnp.int32) % 2
    last_index = jnp.full((1,), N_BLK - 1, jnp.int32)
    return jnp.where(parity == 1, last_index, 2 * halfway).astype(jnp.int32)


def draw_prefix_key_cache(key, part):
    starting_point = jnp.clip(jax.random.normal(jax.random.fold_in(key, 1), (CB, N_BLK, SPAN_LENGTH, MEMORY_GROUPS * FEATURE_DIM), jnp.float32), -6.0, 6.0)
    return starting_point.astype(jnp.bfloat16)


def draw_probe_vectors(key, part):
    starting_point = jnp.clip(2.0 * jax.random.normal(jax.random.fold_in(key, 4), (OPEN_ON_LANE, N_BLK, SPAN_LENGTH, QUERY_GROUPS * FEATURE_DIM), jnp.float32), -12.0, 12.0)
    return starting_point.astype(jnp.bfloat16)


def touch_ends(values, rng, smallest, high):
    longest = values.shape.index(max(values.shape))
    spots = []
    for shift in (0, 1):
        where = [jax.random.randint(jax.random.fold_in(rng, axis), (), 0, length) for axis, length in enumerate(values.shape)]
        where[longest] = (where[longest] + shift) % values.shape[longest]
        spots.append(tuple(where))
    return values.at[spots[0]].set(smallest).at[spots[1]].set(high)


def level_of(rng, shape, pieces, smallest, high):
    factor_of, own = 1.0, jax.random.fold_in(rng, 6)
    for position, shards_of in pieces:
        heights = jnp.exp(jax.random.uniform(jax.random.fold_in(own, position), (shards_of,), jnp.float32, smallest / len(pieces), high / len(pieces)))
        factor_of = factor_of * jnp.repeat(heights, shape[position] // shards_of).reshape([-1 if axis == position else 1 for axis in range(len(shape))])
    return factor_of


def bell_draw(own_key, dims, spread, reach, cuts=(), kind=jnp.bfloat16):
    array = spread * jax.random.normal(own_key, dims, jnp.float32)
    if cuts:
        array = array * level_of(own_key, dims, cuts, -0.22, 0.18)
    return jnp.clip(array, -reach, reach).astype(kind)


def setup_inputs(seed: int = 0, part: int = 0) -> dict:
    seeds = jax.random.split(jax.random.key(seed), 14)
    own_keys = jax.random.split(jax.random.fold_in(seeds[13], part), 14)
    probe_vectors = draw_probe_vectors(jax.random.fold_in(jax.random.fold_in(seeds[13], part), 71), part)
    unsettled_lookups = bell_draw(own_keys[1], (OPEN_ON_LANE, N_BLK, SPAN_LENGTH, MEMORY_GROUPS * FEATURE_DIM), 1.0, 6.0, ((1, 8), (3, 2)))
    unsettled_payloads = bell_draw(own_keys[2], (OPEN_ON_LANE, N_BLK, SPAN_LENGTH, MEMORY_GROUPS * FEATURE_DIM), 1.0, 6.0, ((1, 8), (3, 2)))
    uncover_ordering = jax.vmap(lambda own: jax.random.permutation(own, SPAN_LENGTH))(jax.random.split(own_keys[3], OPEN_ON_LANE * N_BLK)).reshape((OPEN_ON_LANE, N_BLK, SPAN_LENGTH)).astype(jnp.int32)
    rounds_finished = touch_ends(jax.random.randint(own_keys[4], (OPEN_ON_LANE, N_BLK), 0, DENOISE_ROUNDS), jax.random.fold_in(own_keys[4], 1), 0, DENOISE_ROUNDS - 1).astype(jnp.int32)
    random_entry_choice = touch_ends(jax.random.randint(own_keys[5], (OPEN_ON_LANE, N_BLK, SPAN_LENGTH), 0, RANDOM_ROWS), jax.random.fold_in(own_keys[5], 1), 0, RANDOM_ROWS - 1).astype(jnp.int32)
    noise_token_keys = bell_draw(seeds[6], (RANDOM_ROWS, MEMORY_GROUPS * FEATURE_DIM), 1.0, 6.0, ((1, 2),))
    noise_token_values = bell_draw(seeds[7], (RANDOM_ROWS, MEMORY_GROUPS * FEATURE_DIM), 1.0, 6.0, ((1, 2),))
    prefix_key_cache = draw_prefix_key_cache(jax.random.fold_in(jax.random.fold_in(seeds[13], part), 71), part)
    prefix_value_cache = bell_draw(own_keys[9], (CB, N_BLK, SPAN_LENGTH, MEMORY_GROUPS * FEATURE_DIM), 1.0, 6.0, ((1, 8), (3, 2)))
    completed_keys = bell_draw(own_keys[10], (N_BLK, SPAN_LENGTH, MEMORY_GROUPS * FEATURE_DIM), 1.0, 6.0, ((0, 8), (2, 2)))
    completed_values = bell_draw(own_keys[11], (N_BLK, SPAN_LENGTH, MEMORY_GROUPS * FEATURE_DIM), 1.0, 6.0, ((0, 8), (2, 2)))
    committing_index = draw_committing_index(jax.random.fold_in(jax.random.fold_in(seeds[13], part), 71), part)
    return dict(probe_vectors=probe_vectors, unsettled_lookups=unsettled_lookups, unsettled_payloads=unsettled_payloads, uncover_ordering=uncover_ordering, rounds_finished=rounds_finished, random_entry_choice=random_entry_choice, noise_token_keys=noise_token_keys, noise_token_values=noise_token_values, prefix_key_cache=prefix_key_cache, prefix_value_cache=prefix_value_cache, completed_keys=completed_keys, completed_values=completed_values, committing_index=committing_index)


def reference(probe_vectors, unsettled_lookups, unsettled_payloads, uncover_ordering, rounds_finished, random_entry_choice, noise_token_keys, noise_token_values, prefix_key_cache, prefix_value_cache, completed_keys, completed_values, committing_index):
    concealed_flags = uncover_ordering >= UNMASK * rounds_finished[:, :, None]
    onehot = (random_entry_choice[..., None] == jnp.arange(RANDOM_ROWS, dtype=jnp.int32)).astype(jnp.float32)
    blended_lookups = jnp.einsum('sjtn,nc->sjtc', onehot, noise_token_keys.astype(jnp.float32)).astype(jnp.bfloat16)
    blended_payloads = jnp.einsum('sjtn,nc->sjtc', onehot, noise_token_values.astype(jnp.float32)).astype(jnp.bfloat16)
    own_span_lookups = jnp.where(concealed_flags[..., None], blended_lookups, unsettled_lookups).reshape(OPEN_COUNT, SPAN_LENGTH, MEMORY_GROUPS * FEATURE_DIM)
    own_span_payloads = jnp.where(concealed_flags[..., None], blended_payloads, unsettled_payloads).reshape(OPEN_COUNT, SPAN_LENGTH, MEMORY_GROUPS * FEATURE_DIM)
    prev_keys = jnp.roll(own_span_lookups, 1, axis=0)
    prev_values = jnp.roll(own_span_payloads, 1, axis=0)
    owner = committing_index[0].astype(jnp.int32)
    commit_keys = lax.dynamic_index_in_dim(completed_keys, owner, 0, keepdims=False)
    commit_values = lax.dynamic_index_in_dim(completed_values, owner, 0, keepdims=False)
    prefix_keys = prefix_key_cache.reshape(PREFIX, MEMORY_GROUPS * FEATURE_DIM)
    prefix_values = prefix_value_cache.reshape(PREFIX, MEMORY_GROUPS * FEATURE_DIM)
    group = QUERY_GROUPS // MEMORY_GROUPS
    scale = FEATURE_DIM ** -0.5
    flattened_probes = probe_vectors.reshape(OPEN_COUNT, SPAN_LENGTH, QUERY_GROUPS * FEATURE_DIM)

    def one_block(items):
        query, pk, pv, ok, ov = items
        keys = jnp.concatenate([prefix_keys, commit_keys, pk, ok], axis=0).reshape(-1, MEMORY_GROUPS, FEATURE_DIM).astype(jnp.float32)
        values = jnp.concatenate([prefix_values, commit_values, pv, ov], axis=0).reshape(-1, MEMORY_GROUPS, FEATURE_DIM).astype(jnp.float32)
        qf = query.reshape(SPAN_LENGTH, MEMORY_GROUPS, group, FEATURE_DIM).astype(jnp.float32)
        score = jnp.einsum('tgrd,lgd->grtl', qf, keys) * scale
        top = jnp.max(score, axis=-1, keepdims=True)
        weight = jnp.exp(score - top)
        total = jnp.sum(weight, axis=-1)
        rounded = weight.astype(jnp.bfloat16).astype(jnp.float32)
        summed = jnp.einsum('grtl,lgd->tgrd', rounded, values)
        attended_output = summed / jnp.transpose(total, (2, 0, 1))[..., None]
        return attended_output.reshape(SPAN_LENGTH, QUERY_GROUPS * FEATURE_DIM)

    attended_output = lax.map(one_block, (flattened_probes, prev_keys, prev_values, own_span_lookups, own_span_payloads))
    attended_output = attended_output.reshape(OPEN_ON_LANE, N_BLK, SPAN_LENGTH, QUERY_GROUPS * FEATURE_DIM)
    return jnp.where(concealed_flags[..., None], attended_output, 0.0).astype(jnp.bfloat16)
```

```python
import functools

import jax
import jax.numpy as jnp
from jax import lax
from jax.experimental import pallas as pl
from jax.experimental.pallas import tpu as pltpu
from jax.sharding import PartitionSpec as P

QUERY_GROUPS = 28
MEMORY_GROUPS = 4
FEATURE_DIM = 128
UNMASK = 4
GROUP = QUERY_GROUPS // MEMORY_GROUPS
SCALE = FEATURE_DIM ** (-0.5)


def column(row):
    n = row.shape[1]
    here = lax.broadcasted_iota(jnp.int32, (n, n), 0)
    there = lax.broadcasted_iota(jnp.int32, (n, n), 1)
    return jnp.sum(jnp.where(here == there, row, 0), axis=1, keepdims=True)


def blend_kernel(rounds, order, choice, table_k, table_v, open_k, open_v, own):
    slots, block = open_k.shape[0], open_k.shape[2]
    nrows = table_k.shape[0]
    masks, hots = [], []
    for s in range(slots):
        masks.append(column(jnp.where(order[s] >= UNMASK * rounds[s], 1, 0)) > 0)
        picked = column(choice[s])
        hots.append(
            jnp.where(picked == lax.broadcasted_iota(jnp.int32, (block, nrows), 1), 1.0, 0.0)
        )
    onehot = jnp.concatenate(hots, axis=0).astype(jnp.bfloat16)
    for i, (table, opened) in enumerate(((table_k, open_k), (table_v, open_v))):
        noise = jnp.dot(onehot, table[...], preferred_element_type=jnp.float32)
        for s in range(slots):
            mixed = jnp.where(
                masks[s], noise[s * block : (s + 1) * block], opened[s, 0].astype(jnp.float32)
            )
            own[s, i] = mixed.astype(jnp.bfloat16)


def attend_kernel(
    rounds, order, info, query, near, far, own, prev, out
):
    s = pl.program_id(0)
    slots = pl.num_programs(0)
    block = query.shape[1]
    heads = near.shape[3] // FEATURE_DIM
    came = lax.rem(s + slots - info[0], slots)
    take = info[1] > 0
    mask = column(jnp.where(order[0] >= UNMASK * rounds[s], 1, 0)) > 0
    ones = jnp.ones((FEATURE_DIM,), jnp.bfloat16)
    for h in range(heads):
        cols = slice(h * FEATURE_DIM, (h + 1) * FEATURE_DIM)

        def stack(i):
            last = near.shape[0] - 1
            parts = [near[b, i, :, cols] for b in range(last)]
            parts += [far[b, i, :, cols] for b in range(last)]
            parts.append(jnp.where(take, near[last, i, :, cols], far[last, i, :, cols]))
            parts += [prev[came, i, :, cols], own[0, i, :, cols]]
            return jnp.concatenate(parts, axis=0)

        keys, values = stack(0), stack(1)
        q = jnp.concatenate(
            [
                query[0, :, (h * GROUP + g) * FEATURE_DIM : (h * GROUP + g + 1) * FEATURE_DIM]
                for g in range(GROUP)
            ],
            axis=0,
        )
        score = lax.dot_general(
            q, keys, (((1,), (1,)), ((), ())), preferred_element_type=jnp.float32
        )
        top = jnp.max(score, axis=1, keepdims=True)
        weight = jnp.exp((score - top) * SCALE)
        total = jnp.sum(weight, axis=1, keepdims=True)
        context = jnp.dot(
            weight.astype(jnp.bfloat16), values, preferred_element_type=jnp.float32
        )
        context = context / total
        for g in range(GROUP):
            part = jnp.where(mask, context[g * block : (g + 1) * block], 0.0)
            at = (h * GROUP + g) * FEATURE_DIM
            out[0, :, at : at + FEATURE_DIM] = part.astype(jnp.bfloat16)


def swap(block, axis, bit):
    size = lax.axis_size(axis)
    return lax.ppermute(block, axis, [(i, i ^ bit) for i in range(size)])


def on_device(
    probe_vectors,
    unsettled_lookups,
    unsettled_payloads,
    uncover_ordering,
    rounds_finished,
    random_entry_choice,
    noise_token_keys,
    noise_token_values,
    prefix_key_cache,
    prefix_value_cache,
    completed_keys,
    completed_values,
    committing_index,
):
    slots, block = probe_vectors.shape[0], probe_vectors.shape[2]
    wide = probe_vectors.shape[3]
    width = noise_token_keys.shape[1]
    size = lax.axis_size("blk")
    me = lax.axis_index("blk")
    owner = committing_index[0]
    rounds = rounds_finished.reshape(slots)

    vm = pl.BlockSpec(memory_space=pltpu.VMEM)
    sm = pl.BlockSpec(memory_space=pltpu.SMEM)

    held = jnp.stack(
        [prefix_key_cache.reshape(block, width), prefix_value_cache.reshape(block, width)]
    )[None]
    pick = jnp.stack([completed_keys[0], completed_values[0]])
    own = pl.pallas_call(
        blend_kernel,
        out_shape=jax.ShapeDtypeStruct((slots, 2, block, width), jnp.bfloat16),
        in_specs=[sm] + [vm] * 6,
        out_specs=vm,
        name="blend",
    )(
        rounds,
        uncover_ordering,
        random_entry_choice,
        noise_token_keys,
        noise_token_values,
        unsettled_lookups,
        unsettled_payloads,
    )
    prev = lax.ppermute(own, "blk", [(i, (i + 1) % size) for i in range(size)])
    bit = size // 2
    while True:
        packed = jnp.concatenate([held, pick[None]], axis=0)
        got = swap(packed, "blk", bit)
        same = (owner & bit) == (me & bit)
        if bit == 1:
            break
        held = jnp.concatenate([held, got[:-1]], axis=0)
        pick = jnp.where(same, pick, got[-1])
        bit //= 2

    info = jnp.stack([(me == 0).astype(jnp.int32), same.astype(jnp.int32)])
    whole = lambda a: pl.BlockSpec(a.shape, lambda s: (0,) * a.ndim)
    smem = pl.BlockSpec(memory_space=pltpu.SMEM)
    out = pl.pallas_call(
        attend_kernel,
        grid=(slots,),
        out_shape=jax.ShapeDtypeStruct((slots, block, wide), jnp.bfloat16),
        in_specs=[
            smem,
            pl.BlockSpec((1, 1, block), lambda s: (s, 0, 0)),
            smem,
            pl.BlockSpec((1, block, wide), lambda s: (s, 0, 0)),
            whole(packed),
            whole(got),
            pl.BlockSpec((1, 2, block, width), lambda s: (s, 0, 0, 0)),
            whole(prev),
        ],
        out_specs=pl.BlockSpec((1, block, wide), lambda s: (s, 0, 0)),
        name="attend",
    )(
        rounds,
        uncover_ordering,
        info,
        probe_vectors.reshape(slots, block, wide),
        packed,
        got,
        own,
        prev,
    )
    return out.reshape(slots, 1, block, wide)


def solution(mesh):
    placed = (
        P("groups", "blk", None, "mp"),
        P("groups", "blk", None, "mp"),
        P("groups", "blk", None, "mp"),
        P("groups", "blk", None),
        P("groups", "blk"),
        P("groups", "blk", None),
        P(None, "mp"),
        P(None, "mp"),
        P("groups", "blk", None, "mp"),
        P("groups", "blk", None, "mp"),
        P(("groups", "blk"), None, "mp"),
        P(("groups", "blk"), None, "mp"),
        P("groups"),
    )
    return jax.shard_map(
        on_device,
        mesh=mesh,
        in_specs=placed,
        out_specs=P("groups", "blk", None, "mp"),
        check_vma=False,
    )
```

```python
import math

import jax
import jax.numpy as jnp
from jax import lax
from jax.experimental import pallas as pl
from jax.experimental.pallas import tpu as pltpu
from jax.sharding import PartitionSpec as P


QUERY_GROUPS = 28
MEMORY_GROUPS = 4
FEATURE_DIM = 128
UNMASK = 4
GROUP = QUERY_GROUPS // MEMORY_GROUPS
RATE = FEATURE_DIM ** (-0.5) * math.log2(math.e)

SMALL = 8


def column(row):
    n = row.shape[1]
    here = lax.broadcasted_iota(jnp.int32, (n, n), 0)
    there = lax.broadcasted_iota(jnp.int32, (n, n), 1)
    return jnp.sum(jnp.where(here == there, row, 0), axis=1, keepdims=True)


def blend_kernel(
    rounds, order_at, choice_at, table_k_at, table_v_at, open_k_at, open_v_at, own, *scratch
):
    sources = (order_at, choice_at, table_k_at, table_v_at, open_k_at, open_v_at)
    order, choice, table_k, table_v, open_k, open_v, sems = scratch
    copies = [
        pltpu.make_async_copy(src, dst, sems.at[i])
        for i, (src, dst) in enumerate(zip(sources, scratch))
    ]
    for copy in copies:
        copy.start()
    for copy in copies:
        copy.wait()
    slots, block = open_k.shape[0], open_k.shape[2]
    nrows = table_k.shape[0]
    masks, hots = [], []
    for s in range(slots):
        masks.append(column(jnp.where(order[s] >= UNMASK * rounds[s], 1, 0)) > 0)
        picked = column(choice[s])
        hots.append(
            jnp.where(picked == lax.broadcasted_iota(jnp.int32, (block, nrows), 1), 1.0, 0.0)
        )
    onehot = jnp.concatenate(hots, axis=0).astype(jnp.bfloat16)
    for i, (table, opened) in enumerate(((table_k, open_k), (table_v, open_v))):
        noise = jnp.dot(onehot, table[...], preferred_element_type=jnp.float32)
        for s in range(slots):
            mixed = jnp.where(
                masks[s], noise[s * block : (s + 1) * block], opened[s, 0].astype(jnp.float32)
            )
            own[s, i] = mixed.astype(jnp.bfloat16)


def scores(query, slot, head, keys):
    q = jnp.concatenate(
        [
            query[slot, :, (head * GROUP + g) * FEATURE_DIM : (head * GROUP + g + 1) * FEATURE_DIM]
            for g in range(GROUP)
        ],
        axis=0,
    )
    return lax.dot_general(
        q, keys, (((1,), (1,)), ((), ())), preferred_element_type=jnp.float32
    )


def spread(top, n):
    times = -(-n // top.shape[1])
    return jnp.concatenate([top] * times, axis=1)[:, :n]


def each_slot(slots, blocks, body):
    if blocks <= SMALL:
        for s in range(slots):
            body(s)
    else:
        pl.loop(0, slots)(body)


def grant(blocks):
    return pltpu.CompilerParams(vmem_limit_bytes=20 << 20) if blocks <= SMALL else None


def first_kernel(query, near, own, tops, totals, sums):
    slots, _, _, width = own.shape
    last = near.shape[0] - 1

    def attend(s):
        for h in range(width // FEATURE_DIM):
            cols = slice(h * FEATURE_DIM, (h + 1) * FEATURE_DIM)

            def stack(i):
                parts = [near[b, i, :, cols] for b in range(last)] + [own[s, i, :, cols]]
                return jnp.concatenate(parts, axis=0)

            score = scores(query, s, h, stack(0))
            top = jnp.max(score, axis=1, keepdims=True)
            weight = jnp.exp2((score - top) * RATE)
            tops[s, h] = jnp.broadcast_to(top, tops.shape[2:])
            totals[s, h] = jnp.broadcast_to(
                jnp.sum(weight, axis=1, keepdims=True), totals.shape[2:]
            )
            sums[s, h] = jnp.dot(
                weight.astype(jnp.bfloat16), stack(1), preferred_element_type=jnp.float32
            )

    each_slot(slots, last, attend)


def last_kernel(rounds, order, info, query, near, far, prev, tops, totals, sums, out, made, sems):
    slots, _, block, width = prev.shape
    last = near.shape[0] - 1
    take = info[1] > 0

    def copy_of(s):
        return pltpu.make_async_copy(made.at[s], out.at[s], sems.at[s])

    def attend(s):
        came = lax.rem(s + slots - info[0], slots)
        mask = column(jnp.where(order[s] >= UNMASK * rounds[s], 1, 0)) > 0
        for h in range(width // FEATURE_DIM):
            cols = slice(h * FEATURE_DIM, (h + 1) * FEATURE_DIM)

            def stack(i):
                parts = [far[b, i, :, cols] for b in range(last)]
                parts.append(jnp.where(take, near[last, i, :, cols], far[last, i, :, cols]))
                parts.append(prev[came, i, :, cols])
                return jnp.concatenate(parts, axis=0)

            score = scores(query, s, h, stack(0))
            before = tops[s, h]
            top = jnp.maximum(before, jnp.max(score, axis=1, keepdims=True))
            factor = jnp.exp2((before - top) * RATE)
            weight = jnp.exp2((score - spread(top, score.shape[1])) * RATE)
            total = totals[s, h] * factor + jnp.sum(weight, axis=1, keepdims=True)
            context = sums[s, h] * factor + jnp.dot(
                weight.astype(jnp.bfloat16), stack(1), preferred_element_type=jnp.float32
            )
            context = context / total
            for g in range(GROUP):
                part = jnp.where(mask, context[g * block : (g + 1) * block], 0.0)
                at = (h * GROUP + g) * FEATURE_DIM
                made[s, :, at : at + FEATURE_DIM] = part.astype(jnp.bfloat16)
        copy_of(s).start()

    each_slot(slots, last, attend)
    each_slot(slots, last, lambda s: copy_of(s).wait())


def swap(block, axis, bit):
    size = lax.axis_size(axis)
    return lax.ppermute(block, axis, [(i, i ^ bit) for i in range(size)])


def on_device(
    probe_vectors,
    unsettled_lookups,
    unsettled_payloads,
    uncover_ordering,
    rounds_finished,
    random_entry_choice,
    noise_token_keys,
    noise_token_values,
    prefix_key_cache,
    prefix_value_cache,
    completed_keys,
    completed_values,
    committing_index,
):
    slots, block = probe_vectors.shape[0], probe_vectors.shape[2]
    wide = probe_vectors.shape[3]
    width = noise_token_keys.shape[1]
    size = lax.axis_size("blk")
    me = lax.axis_index("blk")
    owner = committing_index[0]
    rounds = rounds_finished.reshape(slots)

    vm = pl.BlockSpec(memory_space=pltpu.VMEM)
    sm = pl.BlockSpec(memory_space=pltpu.SMEM)

    packed = jnp.stack(
        [
            a.reshape(block, width)
            for a in (prefix_key_cache, prefix_value_cache, completed_keys, completed_values)
        ]
    ).reshape(2, 2, block, width)
    sources = (
        uncover_ordering,
        random_entry_choice,
        noise_token_keys,
        noise_token_values,
        unsettled_lookups,
        unsettled_payloads,
    )
    blend = pl.pallas_call(
        blend_kernel,
        out_shape=jax.ShapeDtypeStruct((slots, 2, block, width), jnp.bfloat16),
        in_specs=[sm] + [pl.BlockSpec(memory_space=pltpu.HBM)] * len(sources),
        out_specs=vm,
        scratch_shapes=[pltpu.VMEM(a.shape, a.dtype) for a in sources]
        + [pltpu.SemaphoreType.DMA((len(sources),))],
        name="blend",
    )
    own = blend(rounds, *sources)
    prev = lax.ppermute(own, "blk", [(i, (i + 1) % size) for i in range(size)])
    bit = size // 2
    while True:
        packed = lax.optimization_barrier(packed)
        got = swap(packed, "blk", bit)
        same = (owner & bit) == (me & bit)
        if bit == 1:
            break
        pick = jnp.where(same, packed[-1:], got[-1:])
        packed = jnp.concatenate([packed[:-1], got[:-1], pick], axis=0)
        bit //= 2

    info = jnp.stack([(me == 0).astype(jnp.int32), same.astype(jnp.int32)])
    heads = width // FEATURE_DIM
    query = probe_vectors.reshape(slots, block, wide)
    part = jax.ShapeDtypeStruct((slots, heads, GROUP * block, FEATURE_DIM), jnp.float32)
    state = pl.pallas_call(
        first_kernel,
        out_shape=[part] * 3,
        in_specs=[vm] * 3,
        out_specs=[vm] * 3,
        compiler_params=grant(size // 2),
        name="early",
    )(query, packed, own)
    out = pl.pallas_call(
        last_kernel,
        out_shape=jax.ShapeDtypeStruct((slots, block, wide), jnp.bfloat16),
        in_specs=[sm, vm, sm] + [vm] * 7,
        out_specs=pl.BlockSpec(memory_space=pl.ANY),
        scratch_shapes=[
            pltpu.VMEM((slots, block, wide), jnp.bfloat16),
            pltpu.SemaphoreType.DMA((slots,)),
        ],
        compiler_params=grant(size // 2),
        name="late",
    )(rounds, uncover_ordering, info, query, packed, got, prev, *state)
    return out.reshape(slots, 1, block, wide)


def solution(mesh):
    placed = (
        P("groups", "blk", None, "mp"),
        P("groups", "blk", None, "mp"),
        P("groups", "blk", None, "mp"),
        P("groups", "blk", None),
        P("groups", "blk"),
        P("groups", "blk", None),
        P(None, "mp"),
        P(None, "mp"),
        P("groups", "blk", None, "mp"),
        P("groups", "blk", None, "mp"),
        P(("groups", "blk"), None, "mp"),
        P(("groups", "blk"), None, "mp"),
        P("groups"),
    )

    return jax.shard_map(
        on_device,
        mesh=mesh,
        in_specs=placed,
        out_specs=P("groups", "blk", None, "mp"),
        check_vma=False,
    )
```

```python
import math

import jax
import jax.numpy as jnp
from jax import lax
from jax.experimental import pallas as pl
from jax.experimental.pallas import tpu as pltpu
from jax.sharding import PartitionSpec as P


QUERY_GROUPS = 28
MEMORY_GROUPS = 4
FEATURE_DIM = 128
UNMASK = 4
GROUP = QUERY_GROUPS // MEMORY_GROUPS
RATE = FEATURE_DIM ** (-0.5) * math.log2(math.e)

SMALL = 8


def column(row):
    n = row.shape[1]
    here = lax.broadcasted_iota(jnp.int32, (n, n), 0)
    there = lax.broadcasted_iota(jnp.int32, (n, n), 1)
    return jnp.sum(jnp.where(here == there, row, 0), axis=1, keepdims=True)


def blend_kernel(
    rounds, turn, order_at, choice_at, table_k_at, table_v_at, open_k_at, open_v_at, own, *scratch
):
    sources = (order_at, choice_at, table_k_at, table_v_at, open_k_at, open_v_at)
    order, choice, table_k, table_v, open_k, open_v, sems = scratch
    copies = [
        pltpu.make_async_copy(src, dst, sems.at[i])
        for i, (src, dst) in enumerate(zip(sources, scratch))
    ]
    for copy in copies:
        copy.start()
    for copy in copies:
        copy.wait()
    slots, block = open_k.shape[0], open_k.shape[2]
    nrows = table_k.shape[0]
    masks, hots = [], []
    for s in range(slots):
        masks.append(column(jnp.where(order[s] >= UNMASK * rounds[s], 1, 0)) > 0)
        picked = column(choice[s])
        hots.append(
            jnp.where(picked == lax.broadcasted_iota(jnp.int32, (block, nrows), 1), 1.0, 0.0)
        )
    onehot = jnp.concatenate(hots, axis=0).astype(jnp.bfloat16)
    for i, (table, opened) in enumerate(((table_k, open_k), (table_v, open_v))):
        noise = jnp.dot(onehot, table[...], preferred_element_type=jnp.float32)
        for s in range(slots):
            mixed = jnp.where(
                masks[s], noise[s * block : (s + 1) * block], opened[s, 0].astype(jnp.float32)
            )
            own[lax.rem(s + turn[0], slots), i] = mixed.astype(jnp.bfloat16)


def scores(query, slot, head, keys):
    q = jnp.concatenate(
        [
            query[slot, :, (head * GROUP + g) * FEATURE_DIM : (head * GROUP + g + 1) * FEATURE_DIM]
            for g in range(GROUP)
        ],
        axis=0,
    )
    return lax.dot_general(
        keys, q, (((1,), (1,)), ((), ())), preferred_element_type=jnp.float32
    )


def gathered(values, weight):
    return lax.dot_general(
        values,
        weight,
        (((0,), (0,)), ((), ())),
        preferred_element_type=jnp.float32,
    )


def staggered(slots, heads, blocks, stages):
    def run(tasks):
        held = {}
        for step in range(len(tasks) + len(stages) - 1):
            for k, stage in enumerate(stages):
                i = step - k
                if 0 <= i < len(tasks):
                    held[i] = stage(*tasks[i], *held.get(i, ()))

    if blocks <= SMALL:
        run([(s, h) for s in range(slots) for h in range(heads)])
    else:
        pl.loop(0, slots)(lambda s: run([(s, h) for h in range(heads)]))


def grant(blocks):
    return pltpu.CompilerParams(vmem_limit_bytes=20 << 20) if blocks <= SMALL else None


def columns(head):
    return slice(head * FEATURE_DIM, (head + 1) * FEATURE_DIM)


def first_kernel(rounds, turn, took, order, query, near, own, tops, totals, sums, keep, mine):
    slots, _, _, width = own.shape
    last = near.shape[0] - 1
    mine[...] = jnp.full(mine.shape, took[0], jnp.int32)

    def stack(s, h, i):
        at = lax.rem(s + turn[0], slots)
        parts = [near[b, i, :, columns(h)] for b in range(last)] + [own[at, i, :, columns(h)]]
        return jnp.concatenate(parts, axis=0)

    def score(s, h):
        if h == 0:
            masked = jnp.where(order[s] >= UNMASK * rounds[s], 1.0, 0.0)
            keep[s] = jnp.concatenate([masked] * GROUP, axis=1)
        return (scores(query, s, h, stack(s, h, 0)),)

    def peak(s, h, score):
        top = jnp.max(score, axis=0, keepdims=True)
        tops[s, h] = top
        return score, top

    def weigh(s, h, score, top):
        weight = jnp.exp2((score - top) * RATE)
        totals[s, h] = jnp.sum(weight, axis=0, keepdims=True)
        return (weight.astype(jnp.bfloat16),)

    def gather(s, h, weight):
        sums[s, h] = gathered(stack(s, h, 1), weight)

    staggered(slots, width // FEATURE_DIM, last, (score, peak, weigh, gather))


def last_kernel(query, near, far, prev, tops, totals, sums, keep, mine, out, made, sems):
    slots, _, block, width = prev.shape
    heads = width // FEATURE_DIM
    last = near.shape[0] - 1
    take = mine[:1, :] > 0

    def copy_of(s):
        return pltpu.make_async_copy(made.at[s], out.at[s], sems.at[s])

    def stack(s, h, i):
        parts = [far[b, i, :, columns(h)] for b in range(last)]
        parts.append(jnp.where(take, near[last, i, :, columns(h)], far[last, i, :, columns(h)]))
        parts.append(prev[s, i, :, columns(h)])
        return jnp.concatenate(parts, axis=0)

    def score(s, h):
        return (scores(query, s, h, stack(s, h, 0)),)

    def peak(s, h, score):
        before = tops[s, h]
        top = jnp.maximum(before, jnp.max(score, axis=0, keepdims=True))
        return score, top, jnp.exp2((before - top) * RATE)

    def weigh(s, h, score, top, factor):
        weight = jnp.exp2((score - top) * RATE)
        total = totals[s, h] * factor + jnp.sum(weight, axis=0, keepdims=True)
        share = jnp.where(keep[s] > 0, 1.0 / total, 0.0)
        return weight.astype(jnp.bfloat16), factor * share, share

    def gather(s, h, weight, old, share):
        return gathered(stack(s, h, 1), weight), old, share

    def finish(s, h, context, old, share):
        context = sums[s, h] * old + context * share
        context = jnp.transpose(context.astype(jnp.bfloat16))
        for g in range(GROUP):
            at = (h * GROUP + g) * FEATURE_DIM
            made[s, :, at : at + FEATURE_DIM] = context[g * block : (g + 1) * block]
        if h == heads - 1:
            copy_of(s).start()

    staggered(slots, heads, last, (score, peak, weigh, gather, finish))
    staggered(slots, 1, last, (lambda s, h: copy_of(s).wait(),))


def swap(block, axis, bit):
    size = lax.axis_size(axis)
    return lax.ppermute(block, axis, [(i, i ^ bit) for i in range(size)])


def on_device(
    probe_vectors,
    unsettled_lookups,
    unsettled_payloads,
    uncover_ordering,
    rounds_finished,
    random_entry_choice,
    noise_token_keys,
    noise_token_values,
    prefix_key_cache,
    prefix_value_cache,
    completed_keys,
    completed_values,
    committing_index,
):
    slots, block = probe_vectors.shape[0], probe_vectors.shape[2]
    wide = probe_vectors.shape[3]
    width = noise_token_keys.shape[1]
    size = lax.axis_size("blk")
    me = lax.axis_index("blk")
    owner = committing_index[0]
    rounds = rounds_finished.reshape(slots)
    turn = (me == size - 1).astype(jnp.int32).reshape(1)

    vm = pl.BlockSpec(memory_space=pltpu.VMEM)
    sm = pl.BlockSpec(memory_space=pltpu.SMEM)

    packed = jnp.stack(
        [
            a.reshape(block, width)
            for a in (prefix_key_cache, prefix_value_cache, completed_keys, completed_values)
        ]
    ).reshape(2, 2, block, width)
    sources = (
        uncover_ordering,
        random_entry_choice,
        noise_token_keys,
        noise_token_values,
        unsettled_lookups,
        unsettled_payloads,
    )
    blend = pl.pallas_call(
        blend_kernel,
        out_shape=jax.ShapeDtypeStruct((slots, 2, block, width), jnp.bfloat16),
        in_specs=[sm] * 2 + [pl.BlockSpec(memory_space=pltpu.HBM)] * len(sources),
        out_specs=vm,
        scratch_shapes=[pltpu.VMEM(a.shape, a.dtype) for a in sources]
        + [pltpu.SemaphoreType.DMA((len(sources),))],
        name="blend",
    )
    own = blend(rounds, turn, *sources)
    prev = lax.ppermute(own, "blk", [(i, (i + 1) % size) for i in range(size)])
    bits = [1 << b for b in reversed(range(size.bit_length() - 1))]
    bits[-2:] = bits[:-3:-1]
    for hop, bit in enumerate(bits):
        packed = lax.optimization_barrier(packed)
        got = swap(packed, "blk", bit)
        same = (owner & bit) == (me & bit)
        if hop < len(bits) - 1:
            pick = jnp.where(same, packed[-1:], got[-1:])
            packed = jnp.concatenate([packed[:-1], got[:-1], pick], axis=0)

    took = same.astype(jnp.int32).reshape(1)
    heads = width // FEATURE_DIM
    query = probe_vectors.reshape(slots, block, wide)
    shapes = [(slots, heads, n, GROUP * block) for n in (1, 1, FEATURE_DIM)]
    shapes = [jax.ShapeDtypeStruct(a, jnp.float32) for a in shapes]
    shapes.append(jax.ShapeDtypeStruct((slots, 1, GROUP * block), jnp.float32))
    shapes.append(jax.ShapeDtypeStruct((8, FEATURE_DIM), jnp.int32))
    state = pl.pallas_call(
        first_kernel,
        out_shape=shapes,
        in_specs=[sm] * 3 + [vm] * 4,
        out_specs=[vm] * len(shapes),
        compiler_params=grant(size // 2),
        name="early",
    )(rounds, turn, took, uncover_ordering, query, packed, own)
    out = pl.pallas_call(
        last_kernel,
        out_shape=jax.ShapeDtypeStruct((slots, block, wide), jnp.bfloat16),
        in_specs=[vm] * (4 + len(shapes)),
        out_specs=pl.BlockSpec(memory_space=pl.ANY),
        scratch_shapes=[
            pltpu.VMEM((slots, block, wide), jnp.bfloat16),
            pltpu.SemaphoreType.DMA((slots,)),
        ],
        compiler_params=grant(size // 2),
        name="late",
    )(query, packed, got, prev, *state)
    return out.reshape(slots, 1, block, wide)


def solution(mesh):
    placed = (
        P("groups", "blk", None, "mp"),
        P("groups", "blk", None, "mp"),
        P("groups", "blk", None, "mp"),
        P("groups", "blk", None),
        P("groups", "blk"),
        P("groups", "blk", None),
        P(None, "mp"),
        P(None, "mp"),
        P("groups", "blk", None, "mp"),
        P("groups", "blk", None, "mp"),
        P(("groups", "blk"), None, "mp"),
        P(("groups", "blk"), None, "mp"),
        P("groups"),
    )

    return jax.shard_map(
        on_device,
        mesh=mesh,
        in_specs=placed,
        out_specs=P("groups", "blk", None, "mp"),
        check_vma=False,
    )
```

```python
import math

import jax
import jax.numpy as jnp
from jax import lax
from jax.experimental import pallas as pl
from jax.experimental.pallas import tpu as pltpu
from jax.sharding import PartitionSpec as P


QUERY_GROUPS = 28
MEMORY_GROUPS = 4
FEATURE_DIM = 128
UNMASK = 4
GROUP = QUERY_GROUPS // MEMORY_GROUPS
RATE = FEATURE_DIM ** (-0.5) * math.log2(math.e)

SMALL = 8


def turn_of():
    return (lax.axis_index("blk") == lax.axis_size("blk") - 1).astype(jnp.int32)


def column(row):
    n = row.shape[1]
    here = lax.broadcasted_iota(jnp.int32, (n, n), 0)
    there = lax.broadcasted_iota(jnp.int32, (n, n), 1)
    return jnp.sum(jnp.where(here == there, row, 0), axis=1, keepdims=True)


def blend_kernel(*refs):
    count = (len(refs) - 3) // 2
    sources, (own, keep), places = refs[:count], refs[count : count + 2], refs[count + 2 : -1]
    sems = refs[-1]
    copies = [
        pltpu.make_async_copy(src, dst, sems.at[i])
        for i, (src, dst) in enumerate(zip(sources, places))
    ]
    for copy in copies:
        copy.start()
    for copy in copies:
        copy.wait()
    rounds, order, choice, table_k, table_v, open_k, open_v = places
    slots, block = open_k.shape[0], open_k.shape[2]
    nrows = table_k.shape[0]
    turn = turn_of()
    masks, hots = [], []
    for s in range(slots):
        mask = jnp.where(order[s] >= UNMASK * rounds[:, s : s + 1], 1, 0)
        keep[s] = jnp.concatenate([mask.astype(jnp.float32)] * GROUP, axis=1)
        masks.append(column(mask) > 0)
        picked = column(choice[s])
        hots.append(
            jnp.where(picked == lax.broadcasted_iota(jnp.int32, (block, nrows), 1), 1.0, 0.0)
        )
    onehot = jnp.concatenate(hots, axis=0).astype(jnp.bfloat16)
    for i, (table, opened) in enumerate(((table_k, open_k), (table_v, open_v))):
        noise = jnp.dot(onehot, table[...], preferred_element_type=jnp.float32)
        for s in range(slots):
            mixed = jnp.where(
                masks[s], noise[s * block : (s + 1) * block], opened[s, 0].astype(jnp.float32)
            )
            own[lax.rem(s + turn, slots), i] = mixed.astype(jnp.bfloat16)


def scores(query, slot, head, keys):
    q = jnp.concatenate(
        [
            query[slot, :, (head * GROUP + g) * FEATURE_DIM : (head * GROUP + g + 1) * FEATURE_DIM]
            for g in range(GROUP)
        ],
        axis=0,
    )
    return lax.dot_general(
        keys, q, (((1,), (1,)), ((), ())), preferred_element_type=jnp.float32
    )


def gathered(values, weight):
    return lax.dot_general(
        values,
        weight,
        (((0,), (0,)), ((), ())),
        preferred_element_type=jnp.float32,
    )


def staggered(slots, heads, blocks, stages):
    def run(tasks):
        held = {}
        for step in range(len(tasks) + len(stages) - 1):
            for k, stage in enumerate(stages):
                i = step - k
                if 0 <= i < len(tasks):
                    held[i] = stage(*tasks[i], *held.get(i, ()))

    if blocks <= SMALL:
        run([(s, h) for s in range(slots) for h in range(heads)])
    else:
        pl.loop(0, slots)(lambda s: run([(s, h) for h in range(heads)]))


def grant(blocks):
    return pltpu.CompilerParams(vmem_limit_bytes=20 << 20) if blocks <= SMALL else None


def columns(head):
    return slice(head * FEATURE_DIM, (head + 1) * FEATURE_DIM)


def first_kernel(took, query, near, own, tops, totals, sums, mine):
    slots, _, _, width = own.shape
    last = near.shape[0] - 1
    mine[...] = jnp.full(mine.shape, took[0], jnp.int32)

    def stack(s, h, i):
        at = lax.rem(s + turn_of(), slots)
        parts = [near[b, i, :, columns(h)] for b in range(last)] + [own[at, i, :, columns(h)]]
        return jnp.concatenate(parts, axis=0)

    def score(s, h):
        return (scores(query, s, h, stack(s, h, 0)),)

    def peak(s, h, score):
        top = jnp.max(score, axis=0, keepdims=True)
        tops[s, h] = top
        return score, top

    def weigh(s, h, score, top):
        weight = jnp.exp2((score - top) * RATE)
        totals[s, h] = jnp.sum(weight, axis=0, keepdims=True)
        return (weight.astype(jnp.bfloat16),)

    def gather(s, h, weight):
        sums[s, h] = gathered(stack(s, h, 1), weight)

    staggered(slots, width // FEATURE_DIM, last, (score, peak, weigh, gather))


def last_kernel(query, near, far, prev, keep, tops, totals, sums, mine, out, made, sems):
    slots, _, block, width = prev.shape
    heads = width // FEATURE_DIM
    last = near.shape[0] - 1
    take = mine[:1, :] > 0

    def copy_of(s):
        return pltpu.make_async_copy(made.at[s], out.at[s], sems.at[s])

    def stack(s, h, i):
        parts = [far[b, i, :, columns(h)] for b in range(last)]
        parts.append(jnp.where(take, near[last, i, :, columns(h)], far[last, i, :, columns(h)]))
        parts.append(prev[s, i, :, columns(h)])
        return jnp.concatenate(parts, axis=0)

    def score(s, h):
        return (scores(query, s, h, stack(s, h, 0)),)

    def peak(s, h, score):
        before = tops[s, h]
        top = jnp.maximum(before, jnp.max(score, axis=0, keepdims=True))
        return score, top, jnp.exp2((before - top) * RATE)

    def weigh(s, h, score, top, factor):
        weight = jnp.exp2((score - top) * RATE)
        total = totals[s, h] * factor + jnp.sum(weight, axis=0, keepdims=True)
        share = jnp.where(keep[s] > 0, 1.0 / total, 0.0)
        return weight.astype(jnp.bfloat16), factor * share, share

    def gather(s, h, weight, old, share):
        return gathered(stack(s, h, 1), weight), old, share

    def finish(s, h, context, old, share):
        context = sums[s, h] * old + context * share
        context = jnp.transpose(context.astype(jnp.bfloat16))
        for g in range(GROUP):
            at = (h * GROUP + g) * FEATURE_DIM
            made[s, :, at : at + FEATURE_DIM] = context[g * block : (g + 1) * block]
        if h == heads - 1:
            copy_of(s).start()

    staggered(slots, heads, last, (score, peak, weigh, gather, finish))
    staggered(slots, 1, last, (lambda s, h: copy_of(s).wait(),))


def swap(block, axis, bit):
    size = lax.axis_size(axis)
    return lax.ppermute(block, axis, [(i, i ^ bit) for i in range(size)])


def on_device(
    probe_vectors,
    unsettled_lookups,
    unsettled_payloads,
    uncover_ordering,
    rounds_finished,
    random_entry_choice,
    noise_token_keys,
    noise_token_values,
    prefix_key_cache,
    prefix_value_cache,
    completed_keys,
    completed_values,
    committing_index,
):
    slots, block = probe_vectors.shape[0], probe_vectors.shape[2]
    wide = probe_vectors.shape[3]
    width = noise_token_keys.shape[1]
    size = lax.axis_size("blk")
    me = lax.axis_index("blk")
    owner = committing_index[0]
    rounds = rounds_finished.reshape(1, slots)

    vm = pl.BlockSpec(memory_space=pltpu.VMEM)
    sm = pl.BlockSpec(memory_space=pltpu.SMEM)

    packed = jnp.stack(
        [
            a.reshape(block, width)
            for a in (prefix_key_cache, prefix_value_cache, completed_keys, completed_values)
        ]
    ).reshape(2, 2, block, width)

    sources = (
        rounds,
        uncover_ordering,
        random_entry_choice,
        noise_token_keys,
        noise_token_values,
        unsettled_lookups,
        unsettled_payloads,
    )
    own, keep = pl.pallas_call(
        blend_kernel,
        out_shape=[
            pltpu.VMEM((slots, 2, block, width), jnp.bfloat16),
            pltpu.VMEM((slots, 1, GROUP * block), jnp.float32),
        ],
        in_specs=[pl.BlockSpec(memory_space=pltpu.HBM)] * len(sources),
        out_specs=[vm] * 2,
        scratch_shapes=[pltpu.VMEM(a.shape, a.dtype) for a in sources]
        + [pltpu.SemaphoreType.DMA((len(sources),))],
        compiler_params=pltpu.CompilerParams(vmem_limit_bytes=4 << 20),
        name="blend",
    )(*(pltpu.with_memory_space_constraint(a, pltpu.HBM) for a in sources))
    prev = lax.ppermute(own, "blk", [(i, (i + 1) % size) for i in range(size)])
    bits = [1 << b for b in reversed(range(size.bit_length() - 1))]
    bits[-2:] = bits[:-3:-1]
    for hop, bit in enumerate(bits):
        packed = lax.optimization_barrier(packed)
        got = swap(packed, "blk", bit)
        same = (owner & bit) == (me & bit)
        if hop < len(bits) - 1:
            pick = jnp.where(same, packed[-1:], got[-1:])
            packed = jnp.concatenate([packed[:-1], got[:-1], pick], axis=0)

    took = same.astype(jnp.int32).reshape(1)
    heads = width // FEATURE_DIM
    query = probe_vectors.reshape(slots, block, wide)
    shapes = [(slots, heads, n, GROUP * block) for n in (1, 1, FEATURE_DIM)]
    shapes = [jax.ShapeDtypeStruct(a, jnp.float32) for a in shapes]
    shapes.append(jax.ShapeDtypeStruct((8, FEATURE_DIM), jnp.int32))
    state = pl.pallas_call(
        first_kernel,
        out_shape=shapes,
        in_specs=[sm] + [vm] * 3,
        out_specs=[vm] * len(shapes),
        compiler_params=grant(size // 2),
        name="early",
    )(took, query, packed, own)
    out = pl.pallas_call(
        last_kernel,
        out_shape=jax.ShapeDtypeStruct((slots, block, wide), jnp.bfloat16),
        in_specs=[vm] * (5 + len(shapes)),
        out_specs=pl.BlockSpec(memory_space=pl.ANY),
        scratch_shapes=[
            pltpu.VMEM((slots, block, wide), jnp.bfloat16),
            pltpu.SemaphoreType.DMA((slots,)),
        ],
        compiler_params=grant(size // 2),
        name="late",
    )(query, packed, got, prev, keep, *state)
    return out.reshape(slots, 1, block, wide)


def solution(mesh):
    placed = (
        P("groups", "blk", None, "mp"),
        P("groups", "blk", None, "mp"),
        P("groups", "blk", None, "mp"),
        P("groups", "blk", None),
        P("groups", "blk"),
        P("groups", "blk", None),
        P(None, "mp"),
        P(None, "mp"),
        P("groups", "blk", None, "mp"),
        P("groups", "blk", None, "mp"),
        P(("groups", "blk"), None, "mp"),
        P(("groups", "blk"), None, "mp"),
        P("groups"),
    )

    return jax.shard_map(
        on_device,
        mesh=mesh,
        in_specs=placed,
        out_specs=P("groups", "blk", None, "mp"),
        check_vma=False,
    )
```

```python
import math

import jax
import jax.numpy as jnp
from jax import lax
from jax.experimental import pallas as pl
from jax.experimental.pallas import tpu as pltpu
from jax.sharding import PartitionSpec as P


QUERY_GROUPS = 28
MEMORY_GROUPS = 4
FEATURE_DIM = 128
UNMASK = 4
GROUP = QUERY_GROUPS // MEMORY_GROUPS
RATE = FEATURE_DIM ** (-0.5) * math.log2(math.e)

SMALL = 4


def turn_of():
    return (lax.axis_index("blk") == lax.axis_size("blk") - 1).astype(jnp.int32)


def column(row):
    n = row.shape[1]
    here = lax.broadcasted_iota(jnp.int32, (n, n), 0)
    there = lax.broadcasted_iota(jnp.int32, (n, n), 1)
    return jnp.sum(jnp.where(here == there, row, 0), axis=1, keepdims=True)


def blend_kernel(*refs):
    count = (len(refs) - 3) // 2
    sources, (own, keep), places = refs[:count], refs[count : count + 2], refs[count + 2 : -1]
    sems = refs[-1]
    copies = [
        pltpu.make_async_copy(src, dst, sems.at[i])
        for i, (src, dst) in enumerate(zip(sources, places))
    ]
    for copy in copies:
        copy.start()
    for copy in copies:
        copy.wait()
    rounds, order, choice, table_k, table_v, open_k, open_v = places
    slots, block = open_k.shape[0], open_k.shape[2]
    nrows = table_k.shape[0]
    turn = turn_of()
    masks, hots = [], []
    for s in range(slots):
        mask = jnp.where(order[s] >= UNMASK * rounds[:, s : s + 1], 1, 0)
        keep[s] = jnp.concatenate([mask.astype(jnp.float32)] * (lanes(block) // block), axis=1)
        masks.append(column(mask) > 0)
        picked = column(choice[s])
        hots.append(
            jnp.where(picked == lax.broadcasted_iota(jnp.int32, (block, nrows), 1), 1.0, 0.0)
        )
    onehot = jnp.concatenate(hots, axis=0).astype(jnp.bfloat16)
    for i, (table, opened) in enumerate(((table_k, open_k), (table_v, open_v))):
        noise = jnp.dot(onehot, table[...], preferred_element_type=jnp.float32)
        for s in range(slots):
            mixed = jnp.where(
                masks[s], noise[s * block : (s + 1) * block], opened[s, 0].astype(jnp.float32)
            )
            own[lax.rem(s + turn, slots), i] = mixed.astype(jnp.bfloat16)


def lanes(block):
    return -(-GROUP * block // FEATURE_DIM) * FEATURE_DIM


def scores(query, slot, head, keys):
    first = head * GROUP
    order = [first + g % GROUP for g in range(lanes(query.shape[1]) // query.shape[1])]
    q = jnp.concatenate(
        [query[slot, :, g * FEATURE_DIM : (g + 1) * FEATURE_DIM] for g in order], axis=0
    )
    return lax.dot_general(
        keys, q, (((1,), (1,)), ((), ())), preferred_element_type=jnp.float32
    )


def gathered(values, weight):
    ones = jnp.ones((16, values.shape[0]), values.dtype)
    lhs = jnp.concatenate([jnp.transpose(values), ones], axis=0)
    got = jnp.dot(lhs, weight, preferred_element_type=jnp.float32)
    return got[:FEATURE_DIM], got[FEATURE_DIM : FEATURE_DIM + 1]


def staggered(slots, heads, blocks, stages):
    def run(tasks):
        held = {}
        for step in range(-(-len(tasks) // 3) + len(stages) - 1):
            for k, stage in enumerate(stages):
                for i in range(3 * (step - k), 3 * (step - k) + 3):
                    if 0 <= i < len(tasks):
                        held[i] = stage(*tasks[i], *held.get(i, ()))

    if blocks <= SMALL:
        run([(s, h) for s in range(slots) for h in range(heads)])
    else:
        pl.loop(0, slots)(lambda s: run([(s, h) for h in range(heads)]))


def grant(blocks):
    return pltpu.CompilerParams(vmem_limit_bytes=20 << 20) if blocks <= SMALL else None


def columns(head):
    return slice(head * FEATURE_DIM, (head + 1) * FEATURE_DIM)


def first_kernel(took, query, outer, inner, side, own, tops, totals, sums, mine):
    slots, _, _, width = own.shape
    last = side.shape[0]
    mine[...] = jnp.full(mine.shape, took[0], jnp.int32)

    def stack(s, h, i):
        at = lax.rem(s + turn_of(), slots)
        parts = [a[b, i, :, columns(h)] for a in (outer, inner, side) for b in range(last)]
        return jnp.concatenate(parts + [own[at, i, :, columns(h)]], axis=0)

    def score(s, h):
        return (scores(query, s, h, stack(s, h, 0)),)

    def peak(s, h, score):
        top = jnp.max(score, axis=0, keepdims=True)
        tops[s, h] = top
        return score, top

    def weigh(s, h, score, top):
        weight = jnp.exp2((score - top) * RATE)
        return (weight.astype(jnp.bfloat16),)

    def gather(s, h, weight):
        sums[s, h], totals[s, h] = gathered(stack(s, h, 1), weight)

    staggered(slots, width // FEATURE_DIM, last, (score, peak, weigh, gather))


def last_kernel(query, inner, far, prev, keep, tops, totals, sums, mine, out, made, pick, sems):
    slots, _, block, width = prev.shape
    heads = width // FEATURE_DIM
    last = far.shape[0] - 1
    take = mine[:1, :] > 0
    for i in range(2):
        for h in range(heads):
            pick[i, :, columns(h)] = jnp.where(
                take, inner[last, i, :, columns(h)], far[last, i, :, columns(h)]
            )

    def copy_of(s):
        return pltpu.make_async_copy(made.at[s], out.at[s], sems.at[s])

    def stack(s, h, i):
        parts = [far[b, i, :, columns(h)] for b in range(last)]
        parts.append(pick[i, :, columns(h)])
        parts.append(prev[s, i, :, columns(h)])
        return jnp.concatenate(parts, axis=0)

    def score(s, h):
        return (scores(query, s, h, stack(s, h, 0)),)

    def peak(s, h, score):
        before = tops[s, h]
        top = jnp.maximum(before, jnp.max(score, axis=0, keepdims=True))
        return score, top, jnp.exp2((before - top) * RATE)

    def weigh(s, h, score, top, factor):
        weight = jnp.exp2((score - top) * RATE)
        return weight.astype(jnp.bfloat16), factor

    def gather(s, h, weight, factor):
        return *gathered(stack(s, h, 1), weight), factor

    def finish(s, h, context, total, factor):
        total = totals[s, h] * factor + total
        share = jnp.where(keep[s] > 0, 1.0 / total, 0.0)
        old = factor * share
        context = sums[s, h] * old + context * share
        context = jnp.transpose(context.astype(jnp.bfloat16))
        for g in range(GROUP):
            at = (h * GROUP + g) * FEATURE_DIM
            made[s, :, at : at + FEATURE_DIM] = context[g * block : (g + 1) * block]
        if h == heads - 1:
            copy_of(s).start()

    staggered(slots, heads, last, (score, peak, weigh, gather, finish))
    staggered(slots, 1, last, (lambda s, h: copy_of(s).wait(),))


def swap(block, axis, bit):
    size = lax.axis_size(axis)
    return lax.ppermute(block, axis, [(i, i ^ bit) for i in range(size)])


def on_device(
    probe_vectors,
    unsettled_lookups,
    unsettled_payloads,
    uncover_ordering,
    rounds_finished,
    random_entry_choice,
    noise_token_keys,
    noise_token_values,
    prefix_key_cache,
    prefix_value_cache,
    completed_keys,
    completed_values,
    committing_index,
):
    slots, block = probe_vectors.shape[0], probe_vectors.shape[2]
    wide = probe_vectors.shape[3]
    width = noise_token_keys.shape[1]
    size = lax.axis_size("blk")
    me = lax.axis_index("blk")
    owner = committing_index[0]
    rounds = rounds_finished.reshape(1, slots)

    vm = pl.BlockSpec(memory_space=pltpu.VMEM)
    sm = pl.BlockSpec(memory_space=pltpu.SMEM)

    packed = jnp.stack(
        [
            a.reshape(block, width)
            for a in (prefix_key_cache, prefix_value_cache, completed_keys, completed_values)
        ]
    ).reshape(2, 2, block, width)

    sources = (
        rounds,
        uncover_ordering,
        random_entry_choice,
        noise_token_keys,
        noise_token_values,
        unsettled_lookups,
        unsettled_payloads,
    )
    own, keep = pl.pallas_call(
        blend_kernel,
        out_shape=[
            pltpu.VMEM((slots, 2, block, width), jnp.bfloat16),
            pltpu.VMEM((slots, 1, lanes(block)), jnp.float32),
        ],
        in_specs=[pl.BlockSpec(memory_space=pltpu.HBM)] * len(sources),
        out_specs=[vm] * 2,
        scratch_shapes=[pltpu.VMEM(a.shape, a.dtype) for a in sources]
        + [pltpu.SemaphoreType.DMA((len(sources),))],
        compiler_params=pltpu.CompilerParams(vmem_limit_bytes=4 << 20),
        name="blend",
    )(*(pltpu.with_memory_space_constraint(a, pltpu.HBM) for a in sources))
    prev = lax.ppermute(own, "blk", [(i, (i + 1) % size) for i in range(size)])
    bits = [1 << b for b in reversed(range(size.bit_length() - 1))]
    bits = bits[-1:] + bits[:-1]
    for hop, bit in enumerate(bits):
        packed = lax.optimization_barrier(packed)
        if hop == len(bits) - 2:
            outer = packed
            side = swap(outer[:-1], "blk", bits[-1])
        got = swap(packed, "blk", bit)
        same = (owner & bit) == (me & bit)
        if hop < len(bits) - 1:
            pick = jnp.where(same, packed[-1:], got[-1:])
            known = [] if hop == len(bits) - 2 else [packed[:-1]]
            packed = jnp.concatenate(known + [got[:-1], pick], axis=0)

    took = same.astype(jnp.int32).reshape(1)
    heads = width // FEATURE_DIM
    query = probe_vectors.reshape(slots, block, wide)
    shapes = [(slots, heads, n, lanes(block)) for n in (1, 1, FEATURE_DIM)]
    shapes = [jax.ShapeDtypeStruct(a, jnp.float32) for a in shapes]
    shapes.append(jax.ShapeDtypeStruct((8, FEATURE_DIM), jnp.int32))
    state = pl.pallas_call(
        first_kernel,
        out_shape=shapes,
        in_specs=[sm] + [vm] * 5,
        out_specs=[vm] * len(shapes),
        compiler_params=grant(size // 4),
        name="early",
    )(took, query, outer, packed, side, own)
    out = pl.pallas_call(
        last_kernel,
        out_shape=jax.ShapeDtypeStruct((slots, block, wide), jnp.bfloat16),
        in_specs=[vm] * (5 + len(shapes)),
        out_specs=pl.BlockSpec(memory_space=pl.ANY),
        scratch_shapes=[
            pltpu.VMEM((slots, block, wide), jnp.bfloat16),
            pltpu.VMEM((2, block, width), jnp.bfloat16),
            pltpu.SemaphoreType.DMA((slots,)),
        ],
        compiler_params=grant(size // 4),
        name="late",
    )(query, packed, got, prev, keep, *state)
    return out.reshape(slots, 1, block, wide)


def solution(mesh):
    placed = (
        P("groups", "blk", None, "mp"),
        P("groups", "blk", None, "mp"),
        P("groups", "blk", None, "mp"),
        P("groups", "blk", None),
        P("groups", "blk"),
        P("groups", "blk", None),
        P(None, "mp"),
        P(None, "mp"),
        P("groups", "blk", None, "mp"),
        P("groups", "blk", None, "mp"),
        P(("groups", "blk"), None, "mp"),
        P(("groups", "blk"), None, "mp"),
        P("groups"),
    )

    return jax.shard_map(
        on_device,
        mesh=mesh,
        in_specs=placed,
        out_specs=P("groups", "blk", None, "mp"),
        check_vma=False,
    )
```

```python
import math

import jax
import jax.numpy as jnp
from jax import lax
from jax.experimental import pallas as pl
from jax.experimental.pallas import tpu as pltpu
from jax.sharding import PartitionSpec as P


QUERY_GROUPS = 28
MEMORY_GROUPS = 4
FEATURE_DIM = 128
UNMASK = 4
GROUP = QUERY_GROUPS // MEMORY_GROUPS
RATE = FEATURE_DIM ** (-0.5) * math.log2(math.e)

SMALL = 4


def turn_of():
    return (lax.axis_index("blk") == lax.axis_size("blk") - 1).astype(jnp.int32)


def column(row):
    n = row.shape[1]
    here = lax.broadcasted_iota(jnp.int32, (n, n), 0)
    there = lax.broadcasted_iota(jnp.int32, (n, n), 1)
    return jnp.sum(jnp.where(here == there, row, 0), axis=1, keepdims=True)


def blend_kernel(*refs):
    count = (len(refs) - 3) // 2
    sources, (own, keep), places = refs[:count], refs[count : count + 2], refs[count + 2 : -1]
    sems = refs[-1]
    copies = [
        pltpu.make_async_copy(src, dst, sems.at[i])
        for i, (src, dst) in enumerate(zip(sources, places))
    ]
    for copy in copies:
        copy.start()
    for copy in copies:
        copy.wait()
    rounds, order, choice, table_k, table_v, open_k, open_v = places
    slots, block = open_k.shape[0], open_k.shape[2]
    nrows = table_k.shape[0]
    turn = turn_of()
    masks, hots = [], []
    for s in range(slots):
        mask = jnp.where(order[s] >= UNMASK * rounds[:, s : s + 1], 1, 0)
        keep[s] = jnp.concatenate([mask.astype(jnp.float32)] * (lanes(block) // block), axis=1)
        masks.append(column(mask) > 0)
        picked = column(choice[s])
        hots.append(
            jnp.where(picked == lax.broadcasted_iota(jnp.int32, (block, nrows), 1), 1.0, 0.0)
        )
    onehot = jnp.concatenate(hots, axis=0).astype(jnp.bfloat16)
    for i, (table, opened) in enumerate(((table_k, open_k), (table_v, open_v))):
        noise = jnp.dot(onehot, table[...], preferred_element_type=jnp.float32)
        for s in range(slots):
            mixed = jnp.where(
                masks[s], noise[s * block : (s + 1) * block], opened[s, 0].astype(jnp.float32)
            )
            own[lax.rem(s + turn, slots), i] = mixed.astype(jnp.bfloat16)


def lanes(block):
    return -(-GROUP * block // FEATURE_DIM) * FEATURE_DIM


def scores(query, slot, head, keys):
    first = head * GROUP
    order = [first + g % GROUP for g in range(lanes(query.shape[1]) // query.shape[1])]
    q = jnp.concatenate(
        [query[slot, :, g * FEATURE_DIM : (g + 1) * FEATURE_DIM] for g in order], axis=0
    )
    return lax.dot_general(
        keys, q, (((1,), (1,)), ((), ())), preferred_element_type=jnp.float32
    )


def gathered(values, weight):
    ones = jnp.ones((16, values.shape[0]), values.dtype)
    lhs = jnp.concatenate([jnp.transpose(values), ones], axis=0)
    got = jnp.dot(lhs, weight, preferred_element_type=jnp.float32)
    return got[:FEATURE_DIM], got[FEATURE_DIM : FEATURE_DIM + 1]


def staggered(slots, heads, blocks, stages):
    def run(tasks):
        held = {}
        for step in range(-(-len(tasks) // 3) + len(stages) - 1):
            for k, stage in enumerate(stages):
                for i in range(3 * (step - k), 3 * (step - k) + 3):
                    if 0 <= i < len(tasks):
                        held[i] = stage(*tasks[i], *held.get(i, ()))

    if blocks <= SMALL:
        run([(s, h) for s in range(slots) for h in range(heads)])
    else:
        pl.loop(0, slots)(lambda s: run([(s, h) for h in range(heads)]))


def grant(blocks):
    return pltpu.CompilerParams(vmem_limit_bytes=20 << 20) if blocks <= SMALL else None


def columns(head):
    return slice(head * FEATURE_DIM, (head + 1) * FEATURE_DIM)


def first_kernel(took, query, outer, inner, side, own, tops, totals, sums, mine):
    slots, _, _, width = own.shape
    last = side.shape[0]
    mine[...] = jnp.full(mine.shape, took[0], jnp.int32)

    def stack(s, h, i):
        at = lax.rem(s + turn_of(), slots)
        parts = [a[b, i, :, columns(h)] for a in (outer, inner, side) for b in range(last)]
        return jnp.concatenate(parts + [own[at, i, :, columns(h)]], axis=0)

    def score(s, h):
        return (scores(query, s, h, stack(s, h, 0)),)

    def peak(s, h, score):
        top = jnp.max(score, axis=0, keepdims=True)
        tops[s, h] = top
        return score, top

    def weigh(s, h, score, top):
        weight = jnp.exp2((score - top) * RATE)
        return (weight.astype(jnp.bfloat16),)

    def gather(s, h, weight):
        sums[s, h], totals[s, h] = gathered(stack(s, h, 1), weight)

    staggered(slots, width // FEATURE_DIM, last, (score, peak, weigh, gather))


def last_kernel(query, inner, far, prev, keep, tops, totals, sums, mine, out, made, pick, sems):
    slots, _, block, width = prev.shape
    heads = width // FEATURE_DIM
    last = far.shape[0] - 1
    take = mine[:1, :] > 0
    for i in range(2):
        for h in range(heads):
            pick[i, :, columns(h)] = jnp.where(
                take, inner[last, i, :, columns(h)], far[last, i, :, columns(h)]
            )

    def copy_of(s):
        return pltpu.make_async_copy(made.at[s], out.at[s], sems.at[s])

    def stack(s, h, i):
        parts = [far[b, i, :, columns(h)] for b in range(last)]
        parts.append(pick[i, :, columns(h)])
        parts.append(prev[s, i, :, columns(h)])
        return jnp.concatenate(parts, axis=0)

    def score(s, h):
        return (scores(query, s, h, stack(s, h, 0)),)

    def peak(s, h, score):
        before = tops[s, h]
        top = jnp.maximum(before, jnp.max(score, axis=0, keepdims=True))
        return score, top, jnp.exp2((before - top) * RATE)

    def weigh(s, h, score, top, factor):
        weight = jnp.exp2((score - top) * RATE)
        return weight.astype(jnp.bfloat16), factor

    def gather(s, h, weight, factor):
        return *gathered(stack(s, h, 1), weight), factor

    def finish(s, h, context, total, factor):
        total = totals[s, h] * factor + total
        share = jnp.where(keep[s] > 0, 1.0 / total, 0.0)
        old = factor * share
        context = sums[s, h] * old + context * share
        context = jnp.transpose(context.astype(jnp.bfloat16))
        for g in range(GROUP):
            at = (h * GROUP + g) * FEATURE_DIM
            made[s, :, at : at + FEATURE_DIM] = context[g * block : (g + 1) * block]
        if h == heads - 1:
            copy_of(s).start()

    staggered(slots, heads, last, (score, peak, weigh, gather, finish))
    staggered(slots, 1, last, (lambda s, h: copy_of(s).wait(),))


def swap(block, bits):
    size, cores = lax.axis_size("blk"), lax.axis_size("mp")
    pairs = [
        (i * cores + m, (i ^ bits[m % 2]) * cores + m) for i in range(size) for m in range(cores)
    ]
    return lax.ppermute(block, ("blk", "mp"), pairs)


def on_device(
    probe_vectors,
    unsettled_lookups,
    unsettled_payloads,
    uncover_ordering,
    rounds_finished,
    random_entry_choice,
    noise_token_keys,
    noise_token_values,
    prefix_key_cache,
    prefix_value_cache,
    completed_keys,
    completed_values,
    committing_index,
):
    slots, block = probe_vectors.shape[0], probe_vectors.shape[2]
    wide = probe_vectors.shape[3]
    width = noise_token_keys.shape[1]
    size = lax.axis_size("blk")
    me = lax.axis_index("blk")
    owner = committing_index[0]
    rounds = rounds_finished.reshape(1, slots)

    vm = pl.BlockSpec(memory_space=pltpu.VMEM)
    sm = pl.BlockSpec(memory_space=pltpu.SMEM)

    packed = jnp.stack(
        [
            a.reshape(block, width)
            for a in (prefix_key_cache, prefix_value_cache, completed_keys, completed_values)
        ]
    ).reshape(2, 2, block, width)

    sources = (
        rounds,
        uncover_ordering,
        random_entry_choice,
        noise_token_keys,
        noise_token_values,
        unsettled_lookups,
        unsettled_payloads,
    )
    own, keep = pl.pallas_call(
        blend_kernel,
        out_shape=[
            pltpu.VMEM((slots, 2, block, width), jnp.bfloat16),
            pltpu.VMEM((slots, 1, lanes(block)), jnp.float32),
        ],
        in_specs=[pl.BlockSpec(memory_space=pltpu.HBM)] * len(sources),
        out_specs=[vm] * 2,
        scratch_shapes=[pltpu.VMEM(a.shape, a.dtype) for a in sources]
        + [pltpu.SemaphoreType.DMA((len(sources),))],
        compiler_params=pltpu.CompilerParams(vmem_limit_bytes=4 << 20),
        name="blend",
    )(*(pltpu.with_memory_space_constraint(a, pltpu.HBM) for a in sources))
    prev = lax.ppermute(own, "blk", [(i, (i + 1) % size) for i in range(size)])
    bits = [1 << b for b in reversed(range(size.bit_length() - 1))]
    bits = bits[-1:] + bits[:-1]
    other = bits[1:] + bits[:1]
    odd = lax.axis_index("mp") % 2 == 1
    for hop, pair in enumerate(zip(bits, other)):
        bit = jnp.where(odd, pair[1], pair[0])
        packed = lax.optimization_barrier(packed)
        if hop == len(bits) - 2:
            outer = packed
            side = swap(outer[:-1], (bits[-1], other[-1]))
        got = swap(packed, pair)
        same = (owner & bit) == (me & bit)
        if hop < len(bits) - 1:
            pick = jnp.where(same, packed[-1:], got[-1:])
            known = [] if hop == len(bits) - 2 else [packed[:-1]]
            packed = jnp.concatenate(known + [got[:-1], pick], axis=0)

    took = same.astype(jnp.int32).reshape(1)
    heads = width // FEATURE_DIM
    query = probe_vectors.reshape(slots, block, wide)
    shapes = [(slots, heads, n, lanes(block)) for n in (1, 1, FEATURE_DIM)]
    shapes = [jax.ShapeDtypeStruct(a, jnp.float32) for a in shapes]
    shapes.append(jax.ShapeDtypeStruct((8, FEATURE_DIM), jnp.int32))
    state = pl.pallas_call(
        first_kernel,
        out_shape=shapes,
        in_specs=[sm] + [vm] * 5,
        out_specs=[vm] * len(shapes),
        compiler_params=grant(size // 4),
        name="early",
    )(took, query, outer, packed, side, own)
    out = pl.pallas_call(
        last_kernel,
        out_shape=jax.ShapeDtypeStruct((slots, block, wide), jnp.bfloat16),
        in_specs=[vm] * (5 + len(shapes)),
        out_specs=pl.BlockSpec(memory_space=pl.ANY),
        scratch_shapes=[
            pltpu.VMEM((slots, block, wide), jnp.bfloat16),
            pltpu.VMEM((2, block, width), jnp.bfloat16),
            pltpu.SemaphoreType.DMA((slots,)),
        ],
        compiler_params=grant(size // 4),
        name="late",
    )(query, packed, got, prev, keep, *state)
    return out.reshape(slots, 1, block, wide)


def solution(mesh):
    placed = (
        P("groups", "blk", None, "mp"),
        P("groups", "blk", None, "mp"),
        P("groups", "blk", None, "mp"),
        P("groups", "blk", None),
        P("groups", "blk"),
        P("groups", "blk", None),
        P(None, "mp"),
        P(None, "mp"),
        P("groups", "blk", None, "mp"),
        P("groups", "blk", None, "mp"),
        P(("groups", "blk"), None, "mp"),
        P(("groups", "blk"), None, "mp"),
        P("groups"),
    )

    return jax.shard_map(
        on_device,
        mesh=mesh,
        in_specs=placed,
        out_specs=P("groups", "blk", None, "mp"),
        check_vma=False,
    )
```

```python
import math

import jax
import jax.numpy as jnp
from jax import lax
from jax.experimental import pallas as pl
from jax.experimental.pallas import tpu as pltpu
from jax.sharding import PartitionSpec as P


QUERY_GROUPS = 28
MEMORY_GROUPS = 4
FEATURE_DIM = 128
UNMASK = 4
GROUP = QUERY_GROUPS // MEMORY_GROUPS
RATE = FEATURE_DIM ** (-0.5) * math.log2(math.e)

SMALL = 4


def turn_of():
    return (lax.axis_index("blk") == lax.axis_size("blk") - 1).astype(jnp.int32)


def column(row):
    n = row.shape[1]
    here = lax.broadcasted_iota(jnp.int32, (n, n), 0)
    there = lax.broadcasted_iota(jnp.int32, (n, n), 1)
    return jnp.sum(jnp.where(here == there, row, 0), axis=1, keepdims=True)


def pack_kernel(*refs):
    sources, packed, sems = refs[:-2], refs[-2], refs[-1]
    copies = [
        pltpu.make_async_copy(src, packed.at[i // 2, i % 2], sems.at[i])
        for i, src in enumerate(sources)
    ]
    for copy in copies:
        copy.start()
    for copy in copies:
        copy.wait()


def blend_kernel(*refs):
    count = (len(refs) - 3) // 2
    sources, (own, keep), places = refs[:count], refs[count : count + 2], refs[count + 2 : -1]
    sems = refs[-1]
    copies = [
        pltpu.make_async_copy(src, dst, sems.at[i])
        for i, (src, dst) in enumerate(zip(sources, places))
    ]
    for copy in copies:
        copy.start()
    for copy in copies:
        copy.wait()
    rounds, order, choice, table_k, table_v, open_k, open_v = places
    slots, block = open_k.shape[0], open_k.shape[2]
    nrows = table_k.shape[0]
    turn = turn_of()
    masks, hots = [], []
    for s in range(slots):
        mask = jnp.where(order[s] >= UNMASK * rounds[:, s : s + 1], 1, 0)
        keep[s] = jnp.concatenate([mask.astype(jnp.float32)] * (lanes(block) // block), axis=1)
        masks.append(column(mask) > 0)
        picked = column(choice[s])
        hots.append(
            jnp.where(picked == lax.broadcasted_iota(jnp.int32, (block, nrows), 1), 1.0, 0.0)
        )
    onehot = jnp.concatenate(hots, axis=0).astype(jnp.bfloat16)
    for i, (table, opened) in enumerate(((table_k, open_k), (table_v, open_v))):
        noise = jnp.dot(onehot, table[...], preferred_element_type=jnp.float32)
        for s in range(slots):
            mixed = jnp.where(
                masks[s], noise[s * block : (s + 1) * block], opened[s, 0].astype(jnp.float32)
            )
            own[lax.rem(s + turn, slots), i] = mixed.astype(jnp.bfloat16)


def lanes(block):
    return -(-GROUP * block // FEATURE_DIM) * FEATURE_DIM


def scores(query, slot, head, keys):
    first = head * GROUP
    order = [first + g % GROUP for g in range(lanes(query.shape[1]) // query.shape[1])]
    q = jnp.concatenate(
        [query[slot, :, g * FEATURE_DIM : (g + 1) * FEATURE_DIM] for g in order], axis=0
    )
    return lax.dot_general(
        keys, q, (((1,), (1,)), ((), ())), preferred_element_type=jnp.float32
    )


def gathered(values, weight):
    ones = jnp.ones((16, values.shape[0]), values.dtype)
    lhs = jnp.concatenate([jnp.transpose(values), ones], axis=0)
    got = jnp.dot(lhs, weight, preferred_element_type=jnp.float32)
    return got[:FEATURE_DIM], got[FEATURE_DIM : FEATURE_DIM + 1]


def staggered(slots, heads, blocks, stages):
    def run(tasks):
        held = {}
        for step in range(-(-len(tasks) // 3) + len(stages) - 1):
            for k, stage in enumerate(stages):
                for i in range(3 * (step - k), 3 * (step - k) + 3):
                    if 0 <= i < len(tasks):
                        held[i] = stage(*tasks[i], *held.get(i, ()))

    if blocks <= SMALL:
        run([(s, h) for s in range(slots) for h in range(heads)])
    else:
        pl.loop(0, slots)(lambda s: run([(s, h) for h in range(heads)]))


def grant(blocks):
    return pltpu.CompilerParams(vmem_limit_bytes=20 << 20) if blocks <= SMALL else None


def columns(head):
    return slice(head * FEATURE_DIM, (head + 1) * FEATURE_DIM)


def first_kernel(took, query, outer, inner, side, own, tops, totals, sums, mine):
    slots, _, _, width = own.shape
    last = side.shape[0]
    mine[...] = jnp.full(mine.shape, took[0], jnp.int32)

    def stack(s, h, i):
        at = lax.rem(s + turn_of(), slots)
        parts = [a[b, i, :, columns(h)] for a in (outer, inner, side) for b in range(last)]
        return jnp.concatenate(parts + [own[at, i, :, columns(h)]], axis=0)

    def score(s, h):
        return (scores(query, s, h, stack(s, h, 0)),)

    def peak(s, h, score):
        top = jnp.max(score, axis=0, keepdims=True)
        tops[s, h] = top
        return score, top

    def weigh(s, h, score, top):
        weight = jnp.exp2((score - top) * RATE)
        return (weight.astype(jnp.bfloat16),)

    def gather(s, h, weight):
        sums[s, h], totals[s, h] = gathered(stack(s, h, 1), weight)

    staggered(slots, width // FEATURE_DIM, last, (score, peak, weigh, gather))


def last_kernel(query, inner, far, prev, keep, tops, totals, sums, mine, out, made, pick, sems):
    slots, _, block, width = prev.shape
    heads = width // FEATURE_DIM
    last = far.shape[0] - 1
    take = mine[:1, :] > 0
    for i in range(2):
        for h in range(heads):
            pick[i, :, columns(h)] = jnp.where(
                take, inner[last, i, :, columns(h)], far[last, i, :, columns(h)]
            )

    def copy_of(s):
        return pltpu.make_async_copy(made.at[s], out.at[s], sems.at[s])

    def stack(s, h, i):
        parts = [far[b, i, :, columns(h)] for b in range(last)]
        parts.append(pick[i, :, columns(h)])
        parts.append(prev[s, i, :, columns(h)])
        return jnp.concatenate(parts, axis=0)

    def score(s, h):
        return (scores(query, s, h, stack(s, h, 0)),)

    def peak(s, h, score):
        before = tops[s, h]
        top = jnp.maximum(before, jnp.max(score, axis=0, keepdims=True))
        return score, top, jnp.exp2((before - top) * RATE)

    def weigh(s, h, score, top, factor):
        weight = jnp.exp2((score - top) * RATE)
        return weight.astype(jnp.bfloat16), factor

    def gather(s, h, weight, factor):
        return *gathered(stack(s, h, 1), weight), factor

    def finish(s, h, context, total, factor):
        total = totals[s, h] * factor + total
        share = jnp.where(keep[s] > 0, 1.0 / total, 0.0)
        old = factor * share
        context = sums[s, h] * old + context * share
        context = jnp.transpose(context.astype(jnp.bfloat16))
        for g in range(GROUP):
            at = (h * GROUP + g) * FEATURE_DIM
            made[s, :, at : at + FEATURE_DIM] = context[g * block : (g + 1) * block]
        if h == heads - 1:
            copy_of(s).start()

    staggered(slots, heads, last, (score, peak, weigh, gather, finish))
    staggered(slots, 1, last, (lambda s, h: copy_of(s).wait(),))


def swap(block, bits):
    size, cores = lax.axis_size("blk"), lax.axis_size("mp")
    pairs = [
        (i * cores + m, (i ^ bits[m % 2]) * cores + m) for i in range(size) for m in range(cores)
    ]
    return lax.ppermute(block, ("blk", "mp"), pairs)


def on_device(
    probe_vectors,
    unsettled_lookups,
    unsettled_payloads,
    uncover_ordering,
    rounds_finished,
    random_entry_choice,
    noise_token_keys,
    noise_token_values,
    prefix_key_cache,
    prefix_value_cache,
    completed_keys,
    completed_values,
    committing_index,
):
    slots, block = probe_vectors.shape[0], probe_vectors.shape[2]
    wide = probe_vectors.shape[3]
    width = noise_token_keys.shape[1]
    size = lax.axis_size("blk")
    me = lax.axis_index("blk")
    owner = committing_index[0]
    rounds = rounds_finished.reshape(1, slots)

    vm = pl.BlockSpec(memory_space=pltpu.VMEM)
    sm = pl.BlockSpec(memory_space=pltpu.SMEM)

    hbm = pl.BlockSpec(memory_space=pltpu.HBM)
    blocks = [
        a.reshape(block, width)
        for a in (prefix_key_cache, prefix_value_cache, completed_keys, completed_values)
    ]
    packed = pl.pallas_call(
        pack_kernel,
        out_shape=pltpu.VMEM((2, 2, block, width), jnp.bfloat16),
        in_specs=[hbm] * len(blocks),
        out_specs=vm,
        scratch_shapes=[pltpu.SemaphoreType.DMA((len(blocks),))],
        compiler_params=pltpu.CompilerParams(vmem_limit_bytes=4 << 20),
        name="pack",
    )(*(pltpu.with_memory_space_constraint(a, pltpu.HBM) for a in blocks))

    sources = (
        rounds,
        uncover_ordering,
        random_entry_choice,
        noise_token_keys,
        noise_token_values,
        unsettled_lookups,
        unsettled_payloads,
    )
    own, keep = pl.pallas_call(
        blend_kernel,
        out_shape=[
            pltpu.VMEM((slots, 2, block, width), jnp.bfloat16),
            pltpu.VMEM((slots, 1, lanes(block)), jnp.float32),
        ],
        in_specs=[pl.BlockSpec(memory_space=pltpu.HBM)] * len(sources),
        out_specs=[vm] * 2,
        scratch_shapes=[pltpu.VMEM(a.shape, a.dtype) for a in sources]
        + [pltpu.SemaphoreType.DMA((len(sources),))],
        compiler_params=pltpu.CompilerParams(vmem_limit_bytes=4 << 20),
        name="blend",
    )(*(pltpu.with_memory_space_constraint(a, pltpu.HBM) for a in sources))
    prev = lax.ppermute(own, "blk", [(i, (i + 1) % size) for i in range(size)])
    bits = [1 << b for b in reversed(range(size.bit_length() - 1))]
    bits = bits[-1:] + bits[:-1]
    other = bits[1:] + bits[:1]
    odd = lax.axis_index("mp") % 2 == 1
    for hop, pair in enumerate(zip(bits, other)):
        bit = jnp.where(odd, pair[1], pair[0])
        packed = lax.optimization_barrier(packed)
        if hop == len(bits) - 2:
            outer = packed
            side = swap(outer[:-1], (bits[-1], other[-1]))
        got = swap(packed, pair)
        same = (owner & bit) == (me & bit)
        if hop < len(bits) - 1:
            pick = jnp.where(same, packed[-1:], got[-1:])
            known = [] if hop == len(bits) - 2 else [packed[:-1]]
            packed = jnp.concatenate(known + [got[:-1], pick], axis=0)

    took = same.astype(jnp.int32).reshape(1)
    heads = width // FEATURE_DIM
    query = probe_vectors.reshape(slots, block, wide)
    shapes = [(slots, heads, n, lanes(block)) for n in (1, 1, FEATURE_DIM)]
    shapes = [jax.ShapeDtypeStruct(a, jnp.float32) for a in shapes]
    shapes.append(jax.ShapeDtypeStruct((8, FEATURE_DIM), jnp.int32))
    state = pl.pallas_call(
        first_kernel,
        out_shape=shapes,
        in_specs=[sm] + [vm] * 5,
        out_specs=[vm] * len(shapes),
        compiler_params=grant(size // 4),
        name="early",
    )(took, query, outer, packed, side, own)
    out = pl.pallas_call(
        last_kernel,
        out_shape=jax.ShapeDtypeStruct((slots, block, wide), jnp.bfloat16),
        in_specs=[vm] * (5 + len(shapes)),
        out_specs=pl.BlockSpec(memory_space=pl.ANY),
        scratch_shapes=[
            pltpu.VMEM((slots, block, wide), jnp.bfloat16),
            pltpu.VMEM((2, block, width), jnp.bfloat16),
            pltpu.SemaphoreType.DMA((slots,)),
        ],
        compiler_params=grant(size // 4),
        name="late",
    )(query, packed, got, prev, keep, *state)
    return out.reshape(slots, 1, block, wide)


def solution(mesh):
    placed = (
        P("groups", "blk", None, "mp"),
        P("groups", "blk", None, "mp"),
        P("groups", "blk", None, "mp"),
        P("groups", "blk", None),
        P("groups", "blk"),
        P("groups", "blk", None),
        P(None, "mp"),
        P(None, "mp"),
        P("groups", "blk", None, "mp"),
        P("groups", "blk", None, "mp"),
        P(("groups", "blk"), None, "mp"),
        P(("groups", "blk"), None, "mp"),
        P("groups"),
    )

    return jax.shard_map(
        on_device,
        mesh=mesh,
        in_specs=placed,
        out_specs=P("groups", "blk", None, "mp"),
        check_vma=False,
    )
```
